128 devices in a mesh: patch: 16 (over x, z_lo, core), tensor: 8 (over y, z_hi).
Axes of the slice: x: 4, y: 4, z: 4 (z_hi: 2, z_lo: 2; z = z_hi * 2 + z_lo), core: 2. Of those that a mesh axis runs over, the one named last changes fastest.
Arguments:
- query: bfloat16 [8192, 5120], P('patch', 'tensor'), may hold values from -6 to 6
- key_fresh: bfloat16 [8192, 5120], P('patch', 'tensor'), may hold values from -6 to 6
- value_fresh: bfloat16 [8192, 5120], P('patch', 'tensor'), may hold values from -6 to 6
- key_stale: bfloat16 [8192, 5120], P('patch', 'tensor'), may hold values from -6 to 6
- value_stale: bfloat16 [8192, 5120], P('patch', 'tensor'), may hold values from -6 to 6
- out_weight: bfloat16 [5120, 5120], P('tensor'), may hold values from -0.078125 to 0.078125
- residual: bfloat16 [8192, 5120], P('patch', 'tensor'), may hold values from -6 to 6
- gate: float32 [5120], P('tensor'), may hold values from 0.5 to 1.5
Outputs:
- block_out: bfloat16 [8192, 5120], P('patch', 'tensor')
The draws below stay inside these ranges and needn't reach their ends.
All inputs are finite; a program needn't handle non-finite values.
Results may differ from the reference program's by a relative error of at most 0.006.
Values may be sent and summed in bfloat16 or wider, within the bound.
No kernel may reach another device: no remote copies, remote signals or barrier semaphores. Data moves between devices by JAX's collectives and lax.ppermute only.
A program may use at most 128 MiB of HBM per device.

```python
import jax
import jax.numpy as jnp
from jax import lax

D = 5120
HEADS = 40
HD = 128
TOK_DEV = 512
TOKENS = 8192
HEADS_DEV = 5
N_PATCH = 16
N_TENSOR = 8


def draw_query(key, part):
    own_key = jax.random.fold_in(key, 1)
    values = jnp.clip(1.3 * jax.random.normal(own_key, (TOKENS, HEADS * HD), jnp.float32), -6.0, 6.0)
    return values.astype(jnp.bfloat16)


def draw_key_stale(key, part):
    own_key = jax.random.fold_in(key, 2)
    values = jnp.clip(1.3 * jax.random.normal(own_key, (TOKENS, HEADS * HD), jnp.float32), -6.0, 6.0)
    return values.astype(jnp.bfloat16)


def levels(key, dims, split, least, high):
    level, own = 1.0, jax.random.fold_in(key, 6)
    for dim, shards_of in split:
        heights = jnp.exp(jax.random.uniform(jax.random.fold_in(own, dim), (shards_of,), jnp.float32, least / len(split), high / len(split)))
        level = level * jnp.repeat(heights, dims[dim] // shards_of).reshape([-1 if axis == dim else 1 for axis in range(len(dims))])
    return level


def centred(stream_key, shape, scale, limit, split=(), held_as=jnp.bfloat16):
    factor_of = levels(stream_key, shape, split, -0.22, 0.18) if split else 1.0
    values = jax.random.normal(stream_key, shape, jnp.float32) * scale * factor_of
    return jnp.minimum(jnp.maximum(values, -limit), limit).astype(held_as)


def setup_inputs(seed: int = 0) -> dict:
    streams_of = jax.random.split(jax.random.key(seed), 9)
    query = draw_query(jax.random.fold_in(streams_of[8], 71), 0)
    key_fresh = centred(streams_of[1], (TOKENS, HEADS * HD), 1.3, 6.0, ((0, 16), (1, 8)))
    value_fresh = centred(streams_of[2], (TOKENS, HEADS * HD), 1.0, 6.0, ((0, 16), (1, 8)))
    key_stale = draw_key_stale(jax.random.fold_in(streams_of[8], 71), 0)
    value_stale = centred(streams_of[4], (TOKENS, HEADS * HD), 1.0, 6.0, ((0, 16), (1, 8)))
    out_weight = centred(streams_of[5], (HEADS * HD, D), (HEADS * HD) ** -0.5, 0.078125, ((0, 8),))
    residual = centred(streams_of[6], (TOKENS, D), 1.0, 6.0, ((0, 16), (1, 8)))
    gate = jnp.clip(1.0 + 0.1 * jax.random.normal(streams_of[7], (D,), jnp.float32), 0.5, 1.5)
    return {"query": query, "key_fresh": key_fresh, "value_fresh": value_fresh, "key_stale": key_stale, "value_stale": value_stale, "out_weight": out_weight, "residual": residual, "gate": gate}


def reference(query, key_fresh, value_fresh, key_stale, value_stale, out_weight, residual, gate):
    scale = HD ** -0.5

    def heads_first(array):
        return array.reshape(TOKENS, HEADS, HD).transpose(1, 0, 2)

    def one_head(pieces):
        q_head, k_new, v_new, k_old, v_old = pieces

        def one_block(block):
            start = (block * TOK_DEV).astype(jnp.int32)
            q_rows = lax.dynamic_slice_in_dim(q_head, start, TOK_DEV, 0)
            keys = lax.dynamic_update_slice_in_dim(k_old, lax.dynamic_slice_in_dim(k_new, start, TOK_DEV, 0), start, 0)
            values = lax.dynamic_update_slice_in_dim(v_old, lax.dynamic_slice_in_dim(v_new, start, TOK_DEV, 0), start, 0)
            scores = jnp.dot(q_rows, keys.T, preferred_element_type=jnp.float32) * scale
            expo = jnp.exp(scores - jnp.max(scores, axis=-1, keepdims=True))
            total = jnp.sum(expo, axis=-1, keepdims=True)
            mixed = jnp.dot(expo.astype(jnp.bfloat16), values, preferred_element_type=jnp.float32)
            return (mixed / total).astype(jnp.bfloat16)

        return lax.map(one_block, jnp.arange(N_PATCH, dtype=jnp.int32)).reshape(TOKENS, HD)

    stacked = lax.map(one_head, (heads_first(query), heads_first(key_fresh), heads_first(value_fresh), heads_first(key_stale), heads_first(value_stale)))
    attended = stacked.transpose(1, 0, 2).reshape(TOKENS, HEADS * HD)
    group = HEADS_DEV * HD

    def add_group(running, index):
        first = (index * group).astype(jnp.int32)
        part = jnp.dot(lax.dynamic_slice_in_dim(attended, first, group, 1), lax.dynamic_slice_in_dim(out_weight, first, group, 0), preferred_element_type=jnp.float32)
        rounded = lax.optimization_barrier(part.astype(jnp.bfloat16))
        return running + rounded.astype(jnp.float32), None

    projected, _ = lax.scan(add_group, jnp.zeros((TOKENS, D), jnp.float32), jnp.arange(N_TENSOR, dtype=jnp.int32))
    return (residual.astype(jnp.float32) + gate.astype(jnp.float32)[None, :] * projected).astype(jnp.bfloat16)
```

```python
import functools
import math

import jax
import jax.numpy as jnp
from jax import lax
from jax.experimental import pallas as pl
from jax.experimental.pallas import tpu as pltpu
from jax.sharding import PartitionSpec as P


HD = 128
STAT = 16
TO_LOG2 = math.log2(math.e) / math.sqrt(HD)
AXES = ("x", "zl", "c", "y", "zh")
NT = (((1,), (1,)), ((), ()))
TN = (((0,), (0,)), ((), ()))


def ring(n, k):
    return [(i, (i + k) % n) for i in range(n)]


def dot(a, b, dims):
    return lax.dot_general(a, b, dims, preferred_element_type=jnp.float32)


def attend(q, pieces):
    scores = [dot(k, q, NT) for k, _ in pieces]
    top = functools.reduce(jnp.maximum, [jnp.max(s, axis=0, keepdims=True) for s in scores])
    total, mixed = None, None
    for s, (_, v) in zip(scores, pieces, strict=True):
        expo = jnp.exp2((s - top) * TO_LOG2)
        part = jnp.sum(expo, axis=0, keepdims=True)
        out = dot(v, expo.astype(jnp.bfloat16), TN)
        total = part if total is None else total + part
        mixed = out if mixed is None else mixed + out
    return mixed * (1.0 / total), top * TO_LOG2 + jnp.log2(total)


def flash_kernel(own, qa_ref, qb_ref, kv_ref, sib_ref, z_ref, zs_ref, *refs):
    if own:
        kf_ref, vf_ref, oa_ref, ob_ref, stat = refs
    else:
        oa_ref, ob_ref, stat = refs
    h = pl.program_id(0)
    n = qa_ref.shape[0]

    def halves(ref):
        return ref[0:n, :], ref[n : 2 * n, :]

    shared = [halves(sib_ref), halves(z_ref), halves(zs_ref)]
    rows = pl.ds(pl.multiple_of(h * HD, HD), HD)
    for index, (q_ref, o_ref) in enumerate(((qa_ref, oa_ref), (qb_ref, ob_ref))):
        first = (kf_ref[...], vf_ref[...]) if own and index == 1 else halves(kv_ref)
        out, lse = attend(q_ref[...], [first, *shared])
        o_ref[rows, :] = out.astype(jnp.bfloat16)
        stat[index, pl.ds(h, 1), :] = lse

    @pl.when(h == pl.num_programs(0) - 1)
    def _():
        for index, o_ref in enumerate((oa_ref, ob_ref)):
            lse = stat[index]
            high = lse.astype(jnp.bfloat16)
            low = (lse - high.astype(jnp.float32)).astype(jnp.bfloat16)
            o_ref[pl.num_programs(0) * HD : pl.num_programs(0) * HD + STAT, :] = jnp.concatenate([high, low], axis=0)


def flash(qa, qb, kvs, fresh):
    n, width = qa.shape
    heads = width // HD
    q_spec = pl.BlockSpec((n, HD), lambda h: (0, h))
    kv_spec = pl.BlockSpec((2 * n, HD), lambda h: (0, h))
    o_spec = pl.BlockSpec((width + STAT, n), lambda h: (0, 0))
    o_shape = jax.ShapeDtypeStruct((width + STAT, n), jnp.bfloat16)
    return pl.pallas_call(
        functools.partial(flash_kernel, bool(fresh)),
        out_shape=(o_shape, o_shape),
        grid=(heads,),
        in_specs=[q_spec] * 2 + [kv_spec] * len(kvs) + [q_spec] * len(fresh),
        out_specs=(o_spec, o_spec),
        scratch_shapes=[pltpu.VMEM((2, 8, n), jnp.float32)],
        compiler_params=pltpu.CompilerParams(vmem_limit_bytes=56 << 20),
        cost_estimate=pl.CostEstimate(
            flops=4 * 2 * n * 4 * n * width, bytes_accessed=24 * n * width, transcendentals=8 * n * n * heads
        ),
    )(qa, qb, *kvs, *fresh)


def merge_kernel(*refs):
    *parts, out_ref = refs
    width = out_ref.shape[1]
    stats = []
    for ref in parts:
        both = ref[width : width + STAT, :].astype(jnp.float32)
        stats.append(both[0:8] + both[8:16])
    top = functools.reduce(jnp.maximum, stats)
    weights = [jnp.exp2(s - top) for s in stats]
    total = functools.reduce(jnp.add, weights)
    weights = [w * (1.0 / total) for w in weights]
    for h in range(width // HD):
        mixed = None
        for ref, w in zip(parts, weights, strict=True):
            term = ref[h * HD : (h + 1) * HD, :].astype(jnp.float32) * w[h : h + 1, :]
            mixed = term if mixed is None else mixed + term
        out_ref[:, h * HD : (h + 1) * HD] = mixed.T.astype(jnp.bfloat16)


def merge(parts):
    rows, n = parts[0].shape
    return pl.pallas_call(
        merge_kernel,
        out_shape=jax.ShapeDtypeStruct((n, rows - STAT), jnp.bfloat16),
        compiler_params=pltpu.CompilerParams(vmem_limit_bytes=32 << 20),
        cost_estimate=pl.CostEstimate(flops=8 * rows * n, bytes_accessed=10 * rows * n, transcendentals=0),
    )(*parts)


def project_kernel(where, att_ref, other_ref, w_ref, wz_ref, ws_ref, *outs):
    j = pl.program_id(0)
    target = lax.rem(where[0] + j, 4)
    mine = lax.div(target, 2) == where[2]
    other_w = jnp.where(mine, wz_ref[...], ws_ref[...])
    total = jnp.dot(att_ref[...], w_ref[...], preferred_element_type=jnp.float32)
    total = total + jnp.dot(other_ref[...], other_w, preferred_element_type=jnp.float32)
    result = total.astype(jnp.bfloat16)
    for index, out_ref in enumerate(outs):

        @pl.when(j == index)
        def _():
            out_ref[...] = result


def project(where, att, other, w, wz, ws):
    n, width = att.shape
    act = pl.BlockSpec((n, width), lambda j, where: (0, 0))
    half = pl.BlockSpec((width, width), lambda j, where: (lax.rem(where[0] + j, 2), 0))
    out = jax.ShapeDtypeStruct((n, width), jnp.bfloat16)
    return pl.pallas_call(
        project_kernel,
        out_shape=(out,) * 4,
        grid_spec=pltpu.PrefetchScalarGridSpec(
            num_scalar_prefetch=1,
            grid=(4,),
            in_specs=[
                act,
                act,
                pl.BlockSpec((width, width), lambda j, where: (0, lax.rem(where[0] + j, 4) * 2 + where[1])),
                half,
                half,
            ],
            out_specs=(pl.BlockSpec((n, width), lambda j, where: (0, 0)),) * 4,
        ),
        compiler_params=pltpu.CompilerParams(vmem_limit_bytes=40 << 20),
        cost_estimate=pl.CostEstimate(
            flops=16 * n * width * width, bytes_accessed=24 * width * width + 12 * n * width, transcendentals=0
        ),
    )(where, att, other, w, wz, ws)


def block(query, key_fresh, value_fresh, key_stale, value_stale, out_weight, residual, gate):
    width = query.shape[1]
    y, zh, c = lax.axis_index("y"), lax.axis_index("zh"), lax.axis_index("c")
    swap = ring(2, 1)

    kv = jnp.concatenate([key_stale, value_stale], axis=0)
    kv_z = lax.ppermute(kv, "zl", swap)
    q1 = lax.ppermute(query, "x", ring(4, 1))
    q3 = lax.ppermute(query, "x", ring(4, 3))
    q2 = lax.ppermute(query, "x", ring(4, 2))
    kv_s = lax.ppermute(kv, "c", swap)
    kv_zs = lax.ppermute(kv_z, "c", swap)

    sent = [
        lax.dynamic_slice_in_dim(out_weight, ((2 * c + i) * 2 + 1 - zh) * width, width, 1) for i in range(2)
    ]
    w_z = lax.ppermute(jnp.concatenate(sent, axis=0), ("zl", "zh"), [(0, 3), (3, 0), (1, 2), (2, 1)])
    w_s = lax.ppermute(w_z, "c", swap)

    kvs = (kv, kv_s, kv_z, kv_zs)
    o1, o2 = flash(q1, q2, kvs, ())
    o3, o0 = flash(q3, query, kvs, (key_fresh, value_fresh))
    parts = (
        o0, lax.ppermute(o1, "x", ring(4, 3)), lax.ppermute(o2, "x", ring(4, 2)), lax.ppermute(o3, "x", ring(4, 1))
    )
    attended = merge(parts)
    other = lax.ppermute(attended, "zh", swap)
    where = jnp.stack([y, zh, c]).astype(jnp.int32)
    pieces = project(where, attended, other, out_weight, w_z, w_s)
    whole = pieces[0].astype(jnp.float32)
    for j in range(1, 4):
        whole = whole + lax.ppermute(pieces[j], "y", ring(4, j)).astype(jnp.float32)
    return (residual.astype(jnp.float32) + gate[None, :] * whole).astype(jnp.bfloat16)


def solution(mesh):
    fine = jax.sharding.Mesh(mesh.devices.reshape(4, 2, 2, 4, 2), AXES)
    rows, cols = ("x", "zl", "c"), ("y", "zh")
    spec = P(rows, cols)
    in_specs = (spec, spec, spec, spec, spec, P(cols, None), spec, P(cols))
    return jax.shard_map(block, mesh=fine, in_specs=in_specs, out_specs=spec, check_vma=False)
```

```python
import functools
import math

import jax
import jax.numpy as jnp
from jax import lax
from jax.experimental import pallas as pl
from jax.experimental.pallas import tpu as pltpu
from jax.sharding import PartitionSpec as P


HD = 128
STAT = 16
CHUNKS = 2
TO_LOG2 = math.log2(math.e) / math.sqrt(HD)
AXES = ("x", "zl", "c", "y", "zh")
NT = (((1,), (1,)), ((), ()))
TN = (((0,), (0,)), ((), ()))


def ring(n, k):
    return [(i, (i + k) % n) for i in range(n)]


def dot(a, b, dims):
    return lax.dot_general(a, b, dims, preferred_element_type=jnp.float32)


def attend(q, k, v):
    scores = dot(k, q, NT)
    top = jnp.max(scores, axis=0, keepdims=True)
    expo = jnp.exp2((scores - top) * TO_LOG2)
    return dot(v, expo.astype(jnp.bfloat16), TN), jnp.sum(expo, axis=0, keepdims=True), top * TO_LOG2


def attend_all(q, pieces, extra=()):
    raw = [attend(q, k, v) for k, v in pieces]
    tops = [t for _, _, t in raw] + [lse for _, lse in extra]
    top = functools.reduce(jnp.maximum, tops)
    scaled = [(o, total, jnp.exp2(t - top)) for o, total, t in raw] + [(o, 1.0, jnp.exp2(lse - top)) for o, lse in extra]
    total = functools.reduce(jnp.add, [part * w for _, part, w in scaled])
    inverse = 1.0 / total
    out = functools.reduce(jnp.add, [o * (w * inverse) for o, _, w in scaled])
    return out, top + jnp.log2(total)


def halves(ref):
    n = ref.shape[0] // 2
    return ref[0:n, :], ref[n : 2 * n, :]


def early_kernel(n_q, fresh, *refs):
    q_refs, refs = refs[:n_q], refs[n_q:]
    if fresh:
        own, refs = (refs[0][...], refs[1][...]), refs[2:]
    else:
        own, refs = halves(refs[0]), refs[1:]
    pieces = [own, halves(refs[0])]
    outs = refs[1:]
    h = pl.program_id(0)
    for index, q_ref in enumerate(q_refs):
        out, lse = attend_all(q_ref[...], pieces)
        outs[2 * index][...] = out
        outs[2 * index + 1][pl.ds(h, 1), :] = lse


def early(queries, own, sibling):
    n, width = queries[0].shape
    heads = width // HD
    q_spec = pl.BlockSpec((n, HD), lambda h: (0, h))
    kv_spec = pl.BlockSpec((2 * n, HD), lambda h: (0, h))
    count = len(queries)
    return pl.pallas_call(
        functools.partial(early_kernel, count, len(own) == 2),
        out_shape=(
            jax.ShapeDtypeStruct((width, n), jnp.float32),
            jax.ShapeDtypeStruct((8, n), jnp.float32),
        )
        * count,
        grid=(heads,),
        in_specs=[q_spec] * count + ([q_spec] * 2 if len(own) == 2 else [kv_spec]) + [kv_spec],
        out_specs=(pl.BlockSpec((HD, n), lambda h: (h, 0)), pl.BlockSpec((8, n), lambda h: (0, 0))) * count,
        compiler_params=pltpu.CompilerParams(vmem_limit_bytes=40 << 20),
        cost_estimate=pl.CostEstimate(
            flops=count * 8 * n * n * width, bytes_accessed=16 * n * width, transcendentals=count * 2 * n * n * heads
        ),
    )(*queries, *own, sibling)


def late_kernel(qa_ref, qb_ref, z_ref, zs_ref, ea_ref, la_ref, eb_ref, lb_ref, oa_ref, ob_ref, stat):
    h = pl.program_id(0)
    heads = pl.num_programs(0)
    n = qa_ref.shape[0]
    q = jnp.concatenate([qa_ref[...], qb_ref[...]], axis=0)
    before = jnp.concatenate([ea_ref[...], eb_ref[...]], axis=1)
    before_lse = jnp.concatenate([la_ref[pl.ds(h, 1), :], lb_ref[pl.ds(h, 1), :]], axis=1)
    out, lse = attend_all(q, [halves(z_ref), halves(zs_ref)], [(before, before_lse)])
    out = out.astype(jnp.bfloat16)
    rows = pl.ds(pl.multiple_of(h * HD, HD), HD)
    oa_ref[rows, :] = out[:, 0:n]
    ob_ref[rows, :] = out[:, n : 2 * n]
    stat[pl.ds(h, 1), :] = lse

    @pl.when(h == heads - 1)
    def _():
        high = stat[...].astype(jnp.bfloat16)
        low = (stat[...] - high.astype(jnp.float32)).astype(jnp.bfloat16)
        both = jnp.concatenate([high, low], axis=0)
        base = heads * HD
        oa_ref[base : base + STAT, :] = both[:, 0:n]
        ob_ref[base : base + STAT, :] = both[:, n : 2 * n]


def late(chunk, qa, qb, z, zs, ea, eb):
    whole, width = qa.shape
    n = whole // CHUNKS
    heads = width // HD
    q_spec = pl.BlockSpec((n, HD), lambda h: (chunk, h))
    kv_spec = pl.BlockSpec((2 * whole, HD), lambda h: (0, h))
    e_specs = [pl.BlockSpec((HD, n), lambda h: (h, chunk)), pl.BlockSpec((8, n), lambda h: (0, chunk))]
    o_shape = jax.ShapeDtypeStruct((width + STAT, n), jnp.bfloat16)
    return pl.pallas_call(
        late_kernel,
        out_shape=(o_shape, o_shape),
        grid=(heads,),
        in_specs=[q_spec] * 2 + [kv_spec] * 2 + e_specs * 2,
        out_specs=(pl.BlockSpec((width + STAT, n), lambda h: (0, 0)),) * 2,
        scratch_shapes=[pltpu.VMEM((8, 2 * n), jnp.float32)],
        compiler_params=pltpu.CompilerParams(vmem_limit_bytes=40 << 20),
        cost_estimate=pl.CostEstimate(
            flops=16 * n * whole * width, bytes_accessed=20 * n * width, transcendentals=4 * n * whole * heads
        ),
    )(qa, qb, z, zs, *ea, *eb)


def merge_kernel(*refs):
    *parts, out_ref = refs
    width = out_ref.shape[1]
    stats = []
    for ref in parts:
        both = ref[width : width + STAT, :].astype(jnp.float32)
        stats.append(both[0:8] + both[8:16])
    top = functools.reduce(jnp.maximum, stats)
    weights = [jnp.exp2(s - top) for s in stats]
    total = functools.reduce(jnp.add, weights)
    weights = [w * (1.0 / total) for w in weights]
    for h in range(width // HD):
        mixed = None
        for ref, w in zip(parts, weights, strict=True):
            term = ref[h * HD : (h + 1) * HD, :].astype(jnp.float32) * w[h : h + 1, :]
            mixed = term if mixed is None else mixed + term
        out_ref[:, h * HD : (h + 1) * HD] = mixed.T.astype(jnp.bfloat16)


def merge(parts):
    rows, n = parts[0].shape
    return pl.pallas_call(
        merge_kernel,
        out_shape=jax.ShapeDtypeStruct((n, rows - STAT), jnp.bfloat16),
        compiler_params=pltpu.CompilerParams(vmem_limit_bytes=16 << 20),
        cost_estimate=pl.CostEstimate(flops=8 * rows * n, bytes_accessed=10 * rows * n, transcendentals=0),
    )(*parts)


def project_kernel(where, att_ref, other_ref, w_ref, wz_ref, ws_ref, *outs):
    j = pl.program_id(0)
    target = lax.rem(where[0] + j, 4)
    mine = lax.div(target, 2) == where[2]
    other_w = jnp.where(mine, wz_ref[...], ws_ref[...])
    total = jnp.dot(att_ref[...], w_ref[...], preferred_element_type=jnp.float32)
    total = total + jnp.dot(other_ref[...], other_w, preferred_element_type=jnp.float32)
    result = total.astype(jnp.bfloat16)
    for index, out_ref in enumerate(outs):

        @pl.when(j == index)
        def _():
            out_ref[...] = result


def project(where, att, other, w, wz, ws):
    n, width = att.shape
    act = pl.BlockSpec((n, width), lambda j, where: (0, 0))
    half = pl.BlockSpec((width, width), lambda j, where: (lax.rem(where[0] + j, 2), 0))
    out = jax.ShapeDtypeStruct((n, width), jnp.bfloat16)
    return pl.pallas_call(
        project_kernel,
        out_shape=(out,) * 4,
        grid_spec=pltpu.PrefetchScalarGridSpec(
            num_scalar_prefetch=1,
            grid=(4,),
            in_specs=[
                act,
                act,
                pl.BlockSpec((width, width), lambda j, where: (0, lax.rem(where[0] + j, 4) * 2 + where[1])),
                half,
                half,
            ],
            out_specs=(pl.BlockSpec((n, width), lambda j, where: (0, 0)),) * 4,
        ),
        compiler_params=pltpu.CompilerParams(vmem_limit_bytes=40 << 20),
        cost_estimate=pl.CostEstimate(
            flops=16 * n * width * width, bytes_accessed=24 * width * width + 12 * n * width, transcendentals=0
        ),
    )(where, att, other, w, wz, ws)


def block(query, key_fresh, value_fresh, key_stale, value_stale, out_weight, residual, gate):
    width = query.shape[1]
    y, zh, c = lax.axis_index("y"), lax.axis_index("zh"), lax.axis_index("c")
    where = jnp.stack([y, zh, c]).astype(jnp.int32)
    swap = ring(2, 1)

    kv = jnp.concatenate([key_stale, value_stale], axis=0)
    kv_z = lax.ppermute(kv, "zl", swap)
    kv_s = lax.ppermute(kv, "c", swap)
    q1 = lax.ppermute(query, "x", ring(4, 1))
    q3 = lax.ppermute(query, "x", ring(4, 3))
    q2 = lax.ppermute(query, "x", ring(4, 2))
    kv_zs = lax.ppermute(kv_z, "c", swap)

    sent = [
        lax.dynamic_slice_in_dim(out_weight, ((2 * c + i) * 2 + 1 - zh) * width, width, 1) for i in range(2)
    ]
    w_z = lax.ppermute(jnp.concatenate(sent, axis=0), ("zl", "zh"), [(0, 3), (3, 0), (1, 2), (2, 1)])
    w_s = lax.ppermute(w_z, "c", swap)

    e0 = early((query,), (key_fresh, value_fresh), kv_s)
    e1, l1, e3, l3 = early((q1, q3), (kv,), kv_s)
    e2 = early((q2,), (kv,), kv_s)

    results = []
    for i in range(CHUNKS):
        o2, o1 = late(i, q2, q1, kv_z, kv_zs, e2, (e1, l1))
        o3, o0 = late(i, q3, query, kv_z, kv_zs, (e3, l3), e0)
        parts = (
            o0, lax.ppermute(o1, "x", ring(4, 3)), lax.ppermute(o2, "x", ring(4, 2)), lax.ppermute(o3, "x", ring(4, 1))
        )
        attended = merge(parts)
        other = lax.ppermute(attended, "zh", swap)
        pieces = project(where, attended, other, out_weight, w_z, w_s)
        whole = pieces[0].astype(jnp.float32)
        for j in range(1, 4):
            whole = whole + lax.ppermute(pieces[j], "y", ring(4, j)).astype(jnp.float32)
        results.append(whole)
    whole = jnp.concatenate(results, axis=0)
    return (residual.astype(jnp.float32) + gate[None, :] * whole).astype(jnp.bfloat16)


def solution(mesh):
    fine = jax.sharding.Mesh(mesh.devices.reshape(4, 2, 2, 4, 2), AXES)
    rows, cols = ("x", "zl", "c"), ("y", "zh")
    spec = P(rows, cols)
    in_specs = (spec, spec, spec, spec, spec, P(cols, None), spec, P(cols))
    return jax.shard_map(block, mesh=fine, in_specs=in_specs, out_specs=spec, check_vma=False)
```

```python
import functools
import math

import jax
import jax.numpy as jnp
from jax import lax
from jax.experimental import pallas as pl
from jax.experimental.pallas import tpu as pltpu
from jax.sharding import PartitionSpec as P


HD = 128
STAT = 16
CHUNKS = 2
TO_LOG2 = math.log2(math.e) / math.sqrt(HD)
AXES = ("x", "zl", "c", "y", "zh")
NT = (((1,), (1,)), ((), ()))
TN = (((0,), (0,)), ((), ()))


VMEM = pl.BlockSpec(memory_space=pltpu.VMEM)


def ring(n, k):
    return [(i, (i + k) % n) for i in range(n)]


def dot(a, b, dims):
    return lax.dot_general(a, b, dims, preferred_element_type=jnp.float32)


def call(kernel, out_shape, *args, limit, scratch=(), specs=None, flops=0):
    size = sum(x.size * x.dtype.itemsize for x in args)
    return pl.pallas_call(
        kernel,
        out_shape=out_shape,
        in_specs=specs or [VMEM] * len(args),
        out_specs=jax.tree.map(lambda _: VMEM, out_shape),
        scratch_shapes=scratch,
        compiler_params=pltpu.CompilerParams(vmem_limit_bytes=limit << 20),
        cost_estimate=pl.CostEstimate(flops=flops, bytes_accessed=size, transcendentals=0),
    )(*args)


def attend(q, pieces, extra=None):
    scores = [dot(k, q, NT) for k, _ in pieces]
    top = functools.reduce(jnp.maximum, [jnp.max(s, axis=0, keepdims=True) for s in scores])
    expo = [jnp.exp2((s - top) * TO_LOG2) for s in scores]
    total = functools.reduce(jnp.add, [jnp.sum(e, axis=0, keepdims=True) for e in expo])
    out = functools.reduce(
        jnp.add, [dot(v, e.astype(jnp.bfloat16), TN) for e, (_, v) in zip(expo, pieces, strict=True)]
    )
    top = top * TO_LOG2
    if extra is None:
        return out * (1.0 / total), top + jnp.log2(total)
    before, before_lse = extra
    best = jnp.maximum(top, before_lse)
    now, then = jnp.exp2(top - best), jnp.exp2(before_lse - best)
    whole = total * now + then
    inverse = 1.0 / whole
    return out * (now * inverse) + before * (then * inverse), best + jnp.log2(whole)


def head_loop(heads, step):
    def run(h, carry):
        step(h, pl.ds(pl.multiple_of(h * HD, HD), HD))
        return carry

    lax.fori_loop(0, heads, run, 0)


def early_kernel(count, *refs):
    queries, (ka, va, kb, vb), outs = refs[:count], refs[count : count + 4], refs[count + 4 :]
    n = queries[0].shape[0]

    def step(h, at):
        q = jnp.concatenate([r[:, at] for r in queries], axis=0)
        out, lse = attend(q, [(ka[:, at], va[:, at]), (kb[:, at], vb[:, at])])
        for i in range(count):
            outs[2 * i][at, :] = out[:, i * n : (i + 1) * n]
            outs[2 * i + 1][pl.ds(h, 1), :] = lse[:, i * n : (i + 1) * n]

    head_loop(queries[0].shape[1] // HD, step)


def early(queries, *kv):
    n, width = queries[0].shape
    count = len(queries)
    shapes = (jax.ShapeDtypeStruct((width, n), jnp.float32), jax.ShapeDtypeStruct((8, n), jnp.float32)) * count
    return call(
        functools.partial(early_kernel, count), shapes, *queries, *kv, limit=26, flops=count * 8 * n * n * width
    )


def late_kernel(segments, *refs):
    count = len(segments)
    queries, refs = refs[:count], refs[count:]
    before, refs = refs[: 2 * count], refs[2 * count :]
    ka, va, kb, vb = refs[:4]
    outs, stat = refs[4:-1], refs[-1]
    rows = [slice(first, first + n) for first, n in segments]
    width = queries[0].shape[1]

    def spans():
        start = 0
        for (_, n), out_ref in zip(segments, outs, strict=True):
            yield out_ref, slice(start, start + n)
            start += n

    def step(h, at):
        q = jnp.concatenate([r[s, at] for r, s in zip(queries, rows, strict=True)], axis=0)
        old = jnp.concatenate([r[at, s] for r, s in zip(before[::2], rows, strict=True)], axis=1)
        old_lse = jnp.concatenate([r[pl.ds(h, 1), s] for r, s in zip(before[1::2], rows, strict=True)], axis=1)
        out, lse = attend(q, [(ka[:, at], va[:, at]), (kb[:, at], vb[:, at])], (old, old_lse))
        for out_ref, span in spans():
            out_ref[at, :] = out[:, span].astype(jnp.bfloat16)
        stat[pl.ds(h, 1), :] = lse

    head_loop(width // HD, step)
    high = stat[...].astype(jnp.bfloat16)
    low = (stat[...] - high.astype(jnp.float32)).astype(jnp.bfloat16)
    both = jnp.concatenate([high, low], axis=0)
    for out_ref, span in spans():
        out_ref[width : width + STAT, :] = both[:, span]


def late(segments, *kv):
    whole, width = segments[0][0].shape
    spans = tuple((first, n) for _, _, first, n in segments)
    return call(
        functools.partial(late_kernel, spans),
        tuple(jax.ShapeDtypeStruct((width + STAT, n), jnp.bfloat16) for _, n in spans),
        *(q for q, _, _, _ in segments),
        *(part for _, e, _, _ in segments for part in e),
        *kv,
        limit=26,
        scratch=[pltpu.VMEM((8, sum(n for _, n in spans)), jnp.float32)],
        flops=sum(n for _, n in spans) * 8 * whole * width,
    )


def merge_kernel(first, *refs):
    *parts, out_ref = refs
    n, width = out_ref.shape
    own = slice(first, first + n)
    spans = [own] + [slice(0, n)] * (len(parts) - 1)
    stats = []
    for ref, span in zip(parts, spans, strict=True):
        both = ref[width : width + STAT, span].astype(jnp.float32)
        stats.append(both[0:8] + both[8:16])
    top = functools.reduce(jnp.maximum, stats)
    weights = [jnp.exp2(s - top) for s in stats]
    total = functools.reduce(jnp.add, weights)
    weights = [w * (1.0 / total) for w in weights]
    for h in range(width // HD):
        mixed = None
        for ref, span, w in zip(parts, spans, weights, strict=True):
            term = ref[h * HD : (h + 1) * HD, span].astype(jnp.float32) * w[h : h + 1, :]
            mixed = term if mixed is None else mixed + term
        out_ref[:, h * HD : (h + 1) * HD] = mixed.T.astype(jnp.bfloat16)


def merge(first, n, parts):
    shape = jax.ShapeDtypeStruct((n, parts[0].shape[0] - STAT), jnp.bfloat16)
    return call(functools.partial(merge_kernel, first), shape, *parts, limit=8)


def weight_columns(owner_y, owner_zh, width):
    return pl.ds(pl.multiple_of((owner_y * 2 + owner_zh) * width, HD), width)


def parcel_kernel(w_ref, out_ref, sems):
    width = w_ref.shape[0]
    zh, c = lax.axis_index("zh"), lax.axis_index("c")
    for act in ("start", "wait"):
        for i in range(2):
            at = weight_columns(2 * c + i, 1 - zh, width)
            copy = pltpu.make_async_copy(w_ref.at[:, at], out_ref.at[i * width : (i + 1) * width, :], sems.at[i])
            getattr(copy, act)()


def weight_kernel(w_ref, wz_ref, ws_ref, out_ref, sems):
    width = w_ref.shape[0]
    y, zh, c = lax.axis_index("y"), lax.axis_index("zh"), lax.axis_index("c")

    def other_rows(j, ref):
        at = pl.ds(pl.multiple_of(lax.rem(y + j, 2) * width, width), width)
        return pltpu.make_async_copy(ref.at[at, :], out_ref.at[j, width : 2 * width, :], sems.at[4 + j])

    for act in ("start", "wait"):
        for j in range(4):
            owner = lax.rem(y + j, 4)
            at = weight_columns(owner, zh, width)
            copy = pltpu.make_async_copy(w_ref.at[:, at], out_ref.at[j, 0:width, :], sems.at[j])
            getattr(copy, act)()
            mine = lax.div(owner, 2) == c

            @pl.when(mine)
            def _():
                getattr(other_rows(j, wz_ref), act)()

            @pl.when(jnp.logical_not(mine))
            def _():
                getattr(other_rows(j, ws_ref), act)()


def project_kernel(att_ref, other_ref, w_ref, *outs):
    act = jnp.concatenate([att_ref[...], other_ref[...]], axis=1)
    for j, out_ref in enumerate(outs):
        out_ref[...] = jnp.dot(act, w_ref[j], preferred_element_type=jnp.float32).astype(jnp.bfloat16)


def final_kernel(residual_ref, gate_ref, *refs):
    *pieces, out_ref = refs
    n = out_ref.shape[0] // CHUNKS
    for i in range(CHUNKS):
        rows = slice(i * n, (i + 1) * n)
        mine = [r[...].astype(jnp.float32) for r in pieces[i * 4 : (i + 1) * 4]]
        whole = functools.reduce(jnp.add, mine)
        out_ref[rows, :] = (residual_ref[rows, :].astype(jnp.float32) + gate_ref[...] * whole).astype(jnp.bfloat16)


def block(query, key_fresh, value_fresh, key_stale, value_stale, out_weight, residual, gate):
    rows, width = query.shape
    n = rows // CHUNKS
    swap = ring(2, 1)
    hbm = pl.BlockSpec(memory_space=pl.ANY)

    k_z = lax.ppermute(key_stale, "zl", swap)
    v_z = lax.ppermute(value_stale, "zl", swap)
    q1 = lax.ppermute(query, "x", ring(4, 1))
    q3 = lax.ppermute(query, "x", ring(4, 3))
    k_s = lax.ppermute(key_stale, "c", swap)
    v_s = lax.ppermute(value_stale, "c", swap)
    q2 = lax.ppermute(query, "x", ring(4, 2))
    k_zs = lax.ppermute(k_z, "c", swap)
    v_zs = lax.ppermute(v_z, "c", swap)

    parcel = call(
        parcel_kernel,
        jax.ShapeDtypeStruct((2 * width, width), jnp.bfloat16),
        out_weight,
        limit=4,
        specs=[hbm],
        scratch=[pltpu.SemaphoreType.DMA((2,))],
    )
    w_z = lax.ppermute(parcel, ("zl", "zh"), [(0, 3), (3, 0), (1, 2), (2, 1)])
    w_s = lax.ppermute(w_z, "c", swap)

    e0 = early((query,), key_fresh, value_fresh, k_s, v_s)
    e13 = early((q1, q3), key_stale, value_stale, k_s, v_s)
    e2 = early((q2,), key_stale, value_stale, k_s, v_s)
    far = (k_z, v_z, k_zs, v_zs)
    firsts = [i * n for i in range(CHUNKS)]
    pairs = [late([(q1, e13[:2], first, n), (q3, e13[2:], first, n)], *far) for first in firsts]
    middle = late([(q2, e2, first, n) for first in firsts], *far)
    (o0,) = late([(query, e0, 0, rows)], *far)
    weights = call(
        weight_kernel,
        jax.ShapeDtypeStruct((4, 2 * width, width), jnp.bfloat16),
        out_weight,
        w_z,
        w_s,
        limit=10,
        specs=[hbm] * 3,
        scratch=[pltpu.SemaphoreType.DMA((8,))],
    )

    landed = []
    for i in range(CHUNKS):
        o1, o3 = pairs[i]
        parts = (
            o0,
            lax.ppermute(o1, "x", ring(4, 3)),
            lax.ppermute(middle[i], "x", ring(4, 2)),
            lax.ppermute(o3, "x", ring(4, 1)),
        )
        attended = merge(i * n, n, parts)
        other = lax.ppermute(attended, "zh", swap)
        pieces = call(
            project_kernel,
            (jax.ShapeDtypeStruct((n, width), jnp.bfloat16),) * 4,
            attended,
            other,
            weights,
            limit=16,
            flops=16 * n * width * width,
        )
        landed += [pieces[0], *(lax.ppermute(pieces[j], "y", ring(4, j)) for j in range(1, 4))]
    shape = jax.ShapeDtypeStruct((rows, width), jnp.bfloat16)
    return call(final_kernel, shape, residual, gate, *landed, limit=8)


def solution(mesh):
    fine = jax.sharding.Mesh(mesh.devices.reshape(4, 2, 2, 4, 2), AXES)
    rows, cols = ("x", "zl", "c"), ("y", "zh")
    spec = P(rows, cols)
    in_specs = (spec, spec, spec, spec, spec, P(cols, None), spec, P(cols))
    return jax.shard_map(block, mesh=fine, in_specs=in_specs, out_specs=spec, check_vma=False)
```

```python
import functools
import math

import jax
import jax.numpy as jnp
from jax import lax
from jax.experimental import pallas as pl
from jax.experimental.pallas import tpu as pltpu
from jax.sharding import PartitionSpec as P


HD = 128
STAT = 16
CHUNKS = 2
TO_LOG2 = math.log2(math.e) / math.sqrt(HD)
AXES = ("x", "zl", "c", "y", "zh")
NT = (((1,), (1,)), ((), ()))
TN = (((0,), (0,)), ((), ()))


VMEM = pl.BlockSpec(memory_space=pltpu.VMEM)


def ring(n, k):
    return [(i, (i + k) % n) for i in range(n)]


def dot(a, b, dims):
    return lax.dot_general(a, b, dims, preferred_element_type=jnp.float32)


def call(kernel, out_shape, *args, limit, scratch=(), specs=None, flops=0, size=None):
    size = sum(x.size * x.dtype.itemsize for x in args) if size is None else size
    return pl.pallas_call(
        kernel,
        out_shape=out_shape,
        in_specs=specs or [VMEM] * len(args),
        out_specs=jax.tree.map(lambda _: VMEM, out_shape),
        scratch_shapes=scratch,
        compiler_params=pltpu.CompilerParams(vmem_limit_bytes=limit << 20),
        cost_estimate=pl.CostEstimate(flops=flops, bytes_accessed=size, transcendentals=0),
    )(*args)


def attend(q, pieces, extra=None):
    scores = [dot(k, q, NT) for k, _ in pieces]
    top = functools.reduce(jnp.maximum, [jnp.max(s, axis=0, keepdims=True) for s in scores])
    expo = [jnp.exp2((s - top) * TO_LOG2) for s in scores]
    total = functools.reduce(jnp.add, [jnp.sum(e, axis=0, keepdims=True) for e in expo])
    out = functools.reduce(
        jnp.add, [dot(v, e.astype(jnp.bfloat16), TN) for e, (_, v) in zip(expo, pieces, strict=True)]
    )
    top = top * TO_LOG2
    if extra is None:
        return out * (1.0 / total), top + jnp.log2(total)
    before, before_lse = extra
    best = jnp.maximum(top, before_lse)
    now, then = jnp.exp2(top - best), jnp.exp2(before_lse - best)
    whole = total * now + then
    inverse = 1.0 / whole
    return out * (now * inverse) + before * (then * inverse), best + jnp.log2(whole)


def head_loop(heads, step):
    def run(h, carry):
        step(h, pl.ds(pl.multiple_of(h * HD, HD), HD))
        return carry

    lax.fori_loop(0, heads, run, 0)


def early_own_kernel(*refs):
    q, k, v, *rest, q_in, k_in, v_in, sems = refs
    copies = [pltpu.make_async_copy(a, b, sems.at[i]) for i, (a, b) in enumerate(((q, q_in), (k, k_in), (v, v_in)))]
    for copy in copies:
        copy.start()
    for copy in copies:
        copy.wait()
    early_kernel(1, q_in, k_in, v_in, *rest)


def early_kernel(count, *refs):
    queries, (ka, va, kb, vb), outs = refs[:count], refs[count : count + 4], refs[count + 4 :]
    ends = [sum(r.shape[0] for r in queries[: i + 1]) for i in range(count)]

    def step(h, at):
        q = jnp.concatenate([r[:, at] for r in queries], axis=0)
        out, lse = attend(q, [(ka[:, at], va[:, at]), (kb[:, at], vb[:, at])])
        for i in range(count):
            span = slice(ends[i] - queries[i].shape[0], ends[i])
            outs[2 * i][at, :] = out[:, span]
            outs[2 * i + 1][pl.ds(h, 1), :] = lse[:, span]

    head_loop(queries[0].shape[1] // HD, step)


def early(queries, *kv, load=False):
    keys, width = kv[0].shape
    shapes = [
        (jax.ShapeDtypeStruct((width, q.shape[0]), jnp.float32), jax.ShapeDtypeStruct((8, q.shape[0]), jnp.float32))
        for q in queries
    ]
    parts = call(
        early_own_kernel if load else functools.partial(early_kernel, len(queries)),
        tuple(shape for pair in shapes for shape in pair),
        *queries,
        *kv,
        limit=26,
        specs=[pl.BlockSpec(memory_space=pltpu.HBM)] * 3 + [VMEM] * 2 if load else None,
        scratch=[pltpu.VMEM((keys, width), jnp.bfloat16)] * 3 + [pltpu.SemaphoreType.DMA((3,))] if load else (),
        size=0 if load else None,
        flops=sum(q.shape[0] for q in queries) * 8 * keys * width,
    )
    return [tuple(parts[2 * i : 2 * i + 2]) for i in range(len(queries))]


def late_kernel(segments, *refs):
    count = len(segments)
    queries, refs = refs[:count], refs[count:]
    before, refs = refs[: 2 * count], refs[2 * count :]
    ka, va, kb, vb = refs[:4]
    outs, stat = refs[4:-1], refs[-1]
    rows = [slice(first, first + n) for first, n in segments]
    width = queries[0].shape[1]

    def spans():
        start = 0
        for (_, n), out_ref in zip(segments, outs, strict=True):
            yield out_ref, slice(start, start + n)
            start += n

    def step(h, at):
        q = jnp.concatenate([r[s, at] for r, s in zip(queries, rows, strict=True)], axis=0)
        old = jnp.concatenate([r[at, s] for r, s in zip(before[::2], rows, strict=True)], axis=1)
        old_lse = jnp.concatenate([r[pl.ds(h, 1), s] for r, s in zip(before[1::2], rows, strict=True)], axis=1)
        out, lse = attend(q, [(ka[:, at], va[:, at]), (kb[:, at], vb[:, at])], (old, old_lse))
        for out_ref, span in spans():
            out_ref[at, :] = out[:, span].astype(jnp.bfloat16)
        stat[pl.ds(h, 1), :] = lse

    head_loop(width // HD, step)
    high = stat[...].astype(jnp.bfloat16)
    low = (stat[...] - high.astype(jnp.float32)).astype(jnp.bfloat16)
    both = jnp.concatenate([high, low], axis=0)
    for out_ref, span in spans():
        out_ref[width : width + STAT, :] = both[:, span]


def late(segments, *kv):
    whole, width = kv[0].shape
    spans = tuple((first, n) for _, _, first, n in segments)
    return call(
        functools.partial(late_kernel, spans),
        tuple(jax.ShapeDtypeStruct((width + STAT, n), jnp.bfloat16) for _, n in spans),
        *(q for q, _, _, _ in segments),
        *(part for _, e, _, _ in segments for part in e),
        *kv,
        limit=26,
        scratch=[pltpu.VMEM((8, sum(n for _, n in spans)), jnp.float32)],
        flops=sum(n for _, n in spans) * 8 * whole * width,
    )


def merge_kernel(first, *refs):
    *parts, out_ref = refs
    n, width = out_ref.shape
    own = slice(first, first + n)
    spans = [own] + [slice(0, n)] * (len(parts) - 1)
    stats = []
    for ref, span in zip(parts, spans, strict=True):
        both = ref[width : width + STAT, span].astype(jnp.float32)
        stats.append(both[0:8] + both[8:16])
    top = functools.reduce(jnp.maximum, stats)
    weights = [jnp.exp2(s - top) for s in stats]
    total = functools.reduce(jnp.add, weights)
    weights = [w * (1.0 / total) for w in weights]
    for h in range(width // HD):
        mixed = None
        for ref, span, w in zip(parts, spans, weights, strict=True):
            term = ref[h * HD : (h + 1) * HD, span].astype(jnp.float32) * w[h : h + 1, :]
            mixed = term if mixed is None else mixed + term
        out_ref[:, h * HD : (h + 1) * HD] = mixed.T.astype(jnp.bfloat16)


def merge(first, n, parts):
    shape = jax.ShapeDtypeStruct((n, parts[0].shape[0] - STAT), jnp.bfloat16)
    return call(functools.partial(merge_kernel, first), shape, *parts, limit=8)


def weight_columns(owner_y, owner_zh, width):
    return pl.ds(pl.multiple_of((owner_y * 2 + owner_zh) * width, HD), width)


def parcel_kernel(w_ref, out_ref, sems):
    width = w_ref.shape[0]
    zh, c = lax.axis_index("zh"), lax.axis_index("c")
    for act in ("start", "wait"):
        for i in range(2):
            at = weight_columns(2 * c + i, 1 - zh, width)
            copy = pltpu.make_async_copy(w_ref.at[:, at], out_ref.at[i * width : (i + 1) * width, :], sems.at[i])
            getattr(copy, act)()


def weight_kernel(w_ref, wz_ref, ws_ref, out_ref, sems):
    width = w_ref.shape[0]
    y, zh, c = lax.axis_index("y"), lax.axis_index("zh"), lax.axis_index("c")

    def other_rows(j, ref):
        at = pl.ds(pl.multiple_of(lax.rem(y + j, 2) * width, width), width)
        return pltpu.make_async_copy(ref.at[at, :], out_ref.at[j, width : 2 * width, :], sems.at[4 + j])

    for act in ("start", "wait"):
        for j in range(4):
            owner = lax.rem(y + j, 4)
            at = weight_columns(owner, zh, width)
            copy = pltpu.make_async_copy(w_ref.at[:, at], out_ref.at[j, 0:width, :], sems.at[j])
            getattr(copy, act)()
            mine = lax.div(owner, 2) == c

            @pl.when(mine)
            def _():
                getattr(other_rows(j, wz_ref), act)()

            @pl.when(jnp.logical_not(mine))
            def _():
                getattr(other_rows(j, ws_ref), act)()


def relay_kernel(*refs):
    n = refs[0].shape[0] // CHUNKS
    for i in range(CHUNKS):
        refs[CHUNKS + i][...] = refs[i][i * n : (i + 1) * n, :]


def project_own_kernel(att_ref, w_ref, out_ref):
    width = att_ref.shape[1]
    for j in range(4):
        out_ref[j] = jnp.dot(att_ref[...], w_ref[j, 0:width, :], preferred_element_type=jnp.float32)


def project_other_kernel(targets, own_ref, other_ref, w_ref, *outs):
    width = other_ref.shape[1]
    for j, out_ref in zip(targets, outs, strict=True):
        rest = jnp.dot(other_ref[...], w_ref[j, width : 2 * width, :], preferred_element_type=jnp.float32)
        out_ref[...] = (own_ref[j] + rest).astype(jnp.bfloat16)


def project(attended, other, weights):
    n, width = attended.shape
    shape = jax.ShapeDtypeStruct((4, n, width), jnp.float32)
    own = call(project_own_kernel, shape, attended, weights, limit=16, flops=8 * n * width * width)
    pieces = {}
    for targets in ((1, 3), (2, 0)):
        shapes = (jax.ShapeDtypeStruct((n, width), jnp.bfloat16),) * len(targets)
        kernel = functools.partial(project_other_kernel, targets)
        flops = len(targets) * 2 * n * width * width
        outs = call(kernel, shapes, own, other, weights, limit=16, flops=flops)
        pieces.update(zip(targets, outs, strict=True))
    return pieces


def final_kernel(residual_ref, gate_ref, *refs):
    *pieces, out_ref = refs
    n = out_ref.shape[0] // CHUNKS
    for i in range(CHUNKS):
        rows = slice(i * n, (i + 1) * n)
        mine = [r[...].astype(jnp.float32) for r in pieces[i * 4 : (i + 1) * 4]]
        whole = functools.reduce(jnp.add, mine)
        out_ref[rows, :] = (residual_ref[rows, :].astype(jnp.float32) + gate_ref[...] * whole).astype(jnp.bfloat16)


def block(query, key_fresh, value_fresh, key_stale, value_stale, out_weight, residual, gate):
    rows, width = query.shape
    n = rows // CHUNKS
    swap = ring(2, 1)
    hbm = pl.BlockSpec(memory_space=pltpu.HBM)

    query_at, key_at, value_at, weight_at = (
        pltpu.with_memory_space_constraint(x, pltpu.HBM) for x in (query, key_fresh, value_fresh, out_weight)
    )
    k_s = lax.ppermute(key_stale, "c", swap)
    v_s = lax.ppermute(value_stale, "c", swap)
    k_z = lax.ppermute(key_stale, "zl", swap)
    v_z = lax.ppermute(value_stale, "zl", swap)
    q1 = lax.ppermute(query, "x", ring(4, 1))
    q3 = lax.ppermute(query, "x", ring(4, 3))
    k_zs = lax.ppermute(k_z, "c", swap)
    v_zs = lax.ppermute(v_z, "c", swap)
    relayed = call(relay_kernel, (jax.ShapeDtypeStruct((n, width), jnp.bfloat16),) * CHUNKS, q1, q3, limit=4)
    q2 = [lax.ppermute(relayed[i], "x", ring(4, 1 + 2 * i)) for i in range(CHUNKS)]

    parcel = call(
        parcel_kernel,
        jax.ShapeDtypeStruct((2 * width, width), jnp.bfloat16),
        weight_at,
        limit=4,
        specs=[hbm],
        scratch=[pltpu.SemaphoreType.DMA((2,))],
        size=0,
    )
    w_z = lax.ppermute(parcel, ("zl", "zh"), [(0, 3), (3, 0), (1, 2), (2, 1)])
    w_s = lax.ppermute(w_z, "c", swap)

    (e0,) = early((query_at,), key_at, value_at, k_s, v_s, load=True)
    e1, e3 = early((q1, q3), key_stale, value_stale, k_s, v_s)
    e2 = early(q2, key_stale, value_stale, k_s, v_s)
    far = (k_z, v_z, k_zs, v_zs)
    sent = [late([(q1, e1, i * n, n), (q2[i], e2[i], 0, n), (q3, e3, i * n, n)], *far) for i in range(CHUNKS)]
    own = [late([(query, e0, i * n, n)], *far)[0] for i in range(CHUNKS)]
    weights = call(
        weight_kernel,
        jax.ShapeDtypeStruct((4, 2 * width, width), jnp.bfloat16),
        weight_at,
        w_z,
        w_s,
        limit=10,
        specs=[hbm, pl.BlockSpec(memory_space=pl.ANY), pl.BlockSpec(memory_space=pl.ANY)],
        scratch=[pltpu.SemaphoreType.DMA((8,))],
        size=0,
    )

    landed = []
    for i in range(CHUNKS):
        o1, o2, o3 = sent[i]
        parts = (
            own[i],
            lax.ppermute(o1, "x", ring(4, 3)),
            lax.ppermute(o2, "x", ring(4, 2)),
            lax.ppermute(o3, "x", ring(4, 1)),
        )
        attended = merge(0, n, parts)
        other = lax.ppermute(attended, "zh", swap)
        pieces = project(attended, other, weights)
        landed += [pieces[0], *(lax.ppermute(pieces[j], "y", ring(4, j)) for j in range(1, 4))]
    shape = jax.ShapeDtypeStruct((rows, width), jnp.bfloat16)
    return call(final_kernel, shape, residual, gate, *landed, limit=8)


def solution(mesh):
    fine = jax.sharding.Mesh(mesh.devices.reshape(4, 2, 2, 4, 2), AXES)
    rows, cols = ("x", "zl", "c"), ("y", "zh")
    spec = P(rows, cols)
    in_specs = (spec, spec, spec, spec, spec, P(cols, None), spec, P(cols))
    return jax.shard_map(block, mesh=fine, in_specs=in_specs, out_specs=spec, check_vma=False)
```
